512 devices in a mesh: orb: 128 (over z, y, core), grid: 4 (over x).
Axes of the slice: x: 4, y: 8, z: 8, core: 2. Of those that a mesh axis runs over, the one named last changes fastest.
Arguments:
- orbitals: float32 [256, 32, 1024], P('orb', 'grid'), may hold values from -6 to 6
- dielectric: float32 [256, 32, 1024], P('orb', 'grid'), may hold values from 1 to 80
- pair_offsets: int32 [256, 4], replicated, may hold values from 0 to 3, each once within a row
- pair_counts: int32 [256], replicated, may hold values from 1 to 4, as said below
- box_shift: int32 [256], replicated, may hold values from 0 to 8
Outputs:
- exchange_action: float32 [256, 32, 1024], P('orb', 'grid')
The draws below stay inside these ranges and needn't reach their ends.
Inputs may be any that keep to these rules, and one draw needn't show every extreme that they name: `pair_counts`: in each aligned block of 8 orbitals the counts sum to 16, and in each such block the 2 orbitals of one owner (an aligned run of 2 orbitals) all have 4. `pair_offsets`: each row is a permutation of 0 to 3; only its first pair_counts entries name pairs.
All inputs are finite; a program needn't handle non-finite values.
Results may differ from the reference program's by a relative error of at most 0.00013.
Values sent between devices are 32-bit elements; how exact they have to be, the bound alone decides.
No kernel may reach another device: no remote copies, remote signals or barrier semaphores. Data moves between devices by JAX's collectives and lax.ppermute only.
A program may use at most 64 MiB of HBM per device.

```python
import math
import jax
import jax.numpy as jnp
from jax import lax

B = 32
ORB_DEV = 2
PMAX = 4
MEAN_PAIRS = 2
GROUP = 4
SMAX = 8
CYCLES = 2
SWEEPS = 4
ORBITALS = 256


def draw_orbitals(key, part):
    return jnp.clip(jax.random.normal(key, (ORBITALS, B, B * B), jnp.float32), -6.0, 6.0)


def draw_pair_counts(key, part):
    block_size = GROUP * ORB_DEV
    remaining = block_size - ORB_DEV
    surplus = MEAN_PAIRS * block_size - PMAX * ORB_DEV - remaining
    group_total = ORBITALS // block_size
    pick_count = max(surplus - 1, 1)

    def one_group(group_key):
        first_key, second_key = jax.random.split(group_key)
        busiest = jax.random.randint(first_key, (), 0, GROUP)
        chosen = jax.random.randint(second_key, (pick_count,), 0, remaining)
        usable = jnp.arange(pick_count)[:, None] < surplus - 1
        extras = jnp.sum(((chosen[:, None] == jnp.arange(remaining)[None, :]) & usable).astype(jnp.int32), axis=0)
        lowest = jnp.argmin(extras)
        extras = extras + (jnp.arange(remaining) == lowest).astype(jnp.int32)
        others = 1 + extras
        position = jnp.arange(block_size)
        holder = position // ORB_DEV
        place_index = jnp.clip(position - ORB_DEV * (holder > busiest).astype(jnp.int32), 0, remaining - 1)
        return jnp.where(holder == busiest, PMAX, others[place_index]).astype(jnp.int32)
    group_keys = jax.random.split(key, group_total)
    return jax.vmap(one_group)(group_keys).reshape(-1).astype(jnp.int32)


def set_ends(drawn, key, least, largest):
    longest = drawn.shape.index(max(drawn.shape))
    spots = []
    for shift in (0, 1):
        where = [jax.random.randint(jax.random.fold_in(key, axis), (), 0, length) for axis, length in enumerate(drawn.shape)]
        where[longest] = (where[longest] + shift) % drawn.shape[longest]
        spots.append(tuple(where))
    return drawn.at[spots[0]].set(least).at[spots[1]].set(largest)


def level_of(rng, dims, pieces, smallest, largest):
    loudness = 1.0
    for axis_at, parts in pieces:
        steps = jax.random.uniform(jax.random.fold_in(jax.random.fold_in(rng, 6), axis_at), (parts,), jnp.float32, smallest / len(pieces), largest / len(pieces))
        loudness = loudness * jnp.repeat(jnp.exp(steps), dims[axis_at] // parts).reshape((-1,) + (1,) * (len(dims) - 1 - axis_at))
    return loudness


def setup_inputs(seed: int = 0) -> dict:
    key_list = jax.random.split(jax.random.key(seed), 6)
    return {
        "orbitals": draw_orbitals(jax.random.fold_in(key_list[5], 71), 0),
        "dielectric": jnp.clip(jnp.exp(math.log(80.0) - 4.3820266 * jax.random.uniform(key_list[1], (ORBITALS, B, B * B), jnp.float32) ** level_of(key_list[1], (ORBITALS, B, B * B), ((0, 128), (1, 4)), -0.2, 0.2)), 1.0, 80.0),
        "pair_offsets": jax.vmap(lambda own: jax.random.permutation(own, PMAX))(jax.random.split(key_list[2], ORBITALS)).reshape((ORBITALS, PMAX)).astype(jnp.int32),
        "pair_counts": draw_pair_counts(jax.random.fold_in(key_list[5], 71), 0),
        "box_shift": set_ends(jax.random.randint(key_list[4], (ORBITALS,), 0, SMAX + 1), jax.random.fold_in(key_list[4], 1), 0, SMAX).astype(jnp.int32),
    }


FOURPI = 4.0 * 3.141592653589793
OMEGA = 0.8


def neighbour_cells(cube):
    padded = jnp.pad(cube, 1)
    return [padded[2:, 1:-1, 1:-1], padded[:-2, 1:-1, 1:-1], padded[1:-1, 2:, 1:-1],
            padded[1:-1, :-2, 1:-1], padded[1:-1, 1:-1, 2:], padded[1:-1, 1:-1, :-2]]


def diagonal_of(eps_cube, level_scale):
    summed = jnp.zeros_like(eps_cube)
    for eps_next in neighbour_cells(eps_cube):
        summed = summed + 0.5 * (eps_cube + eps_next)
    return level_scale * summed


def operate(values, eps_cube, diagonal, level_scale):
    weighted = jnp.zeros_like(values)
    for eps_next, val_next in zip(neighbour_cells(eps_cube), neighbour_cells(values)):
        weighted = weighted + 0.5 * (eps_cube + eps_next) * val_next
    return diagonal * values - level_scale * weighted


def coarsen(cube):
    edges = cube.shape
    return cube.reshape(edges[0] // 2, 2, edges[1] // 2, 2, edges[2] // 2, 2).mean(axis=(1, 3, 5))


def refine(cube):
    return jnp.repeat(jnp.repeat(jnp.repeat(cube, 2, axis=0), 2, axis=1), 2, axis=2)


def relaxed_step(values, rhs_level, level_data):
    eps_cube, diagonal, level_scale = level_data
    if values is None:
        return OMEGA * rhs_level / diagonal
    return values + OMEGA * (rhs_level - operate(values, eps_cube, diagonal, level_scale)) / diagonal


def multigrid_cycle(depth_index, values, rhs_level, levels):
    level_data = levels[depth_index]
    if depth_index == len(levels) - 1:
        for sweep_index in range(SWEEPS):
            values = relaxed_step(values, rhs_level, level_data)
        return values
    values = relaxed_step(values, rhs_level, level_data)
    residual = rhs_level - operate(values, level_data[0], level_data[1], level_data[2])
    correction = multigrid_cycle(depth_index + 1, None, coarsen(residual), levels)
    values = values + refine(correction)
    return relaxed_step(values, rhs_level, level_data)


def shift_rows(cube, row_offset):
    padded = jnp.pad(cube, ((0, 0), (SMAX, SMAX), (0, 0)))
    begin = (SMAX + row_offset).astype(jnp.int32)
    return lax.dynamic_slice(padded, (jnp.int32(0), begin, jnp.int32(0)), cube.shape)


def reference(orbitals, dielectric, pair_offsets, pair_counts, box_shift):
    orbital_count = pair_counts.shape[0]
    pair_total = MEAN_PAIRS * orbital_count
    starts = (jnp.cumsum(pair_counts) - pair_counts).astype(jnp.int32)
    serial = jnp.arange(pair_total, dtype=jnp.int32)
    first_orb = (jnp.sum((starts[None, :] <= serial[:, None]).astype(jnp.int32), axis=1) - 1).astype(jnp.int32)
    pair_rank = (serial - starts[first_orb]).astype(jnp.int32)
    second_orb = ((first_orb + 1 + pair_offsets[first_orb, pair_rank]) % orbital_count).astype(jnp.int32)
    orbital_cubes = orbitals.reshape(orbital_count, B, B, B)
    eps_cubes = dielectric.reshape(orbital_count, B, B, B)

    def one_pair(serial_index, summed):
        first_index = first_orb[serial_index]
        second_index = second_orb[serial_index]
        row_offset = (box_shift[first_index] - box_shift[second_index]).astype(jnp.int32)
        phi_first = orbital_cubes[first_index]
        moved = shift_rows(orbital_cubes[second_index], row_offset)
        rhs_fine = FOURPI * (phi_first * moved)
        eps_fine = eps_cubes[first_index]
        eps_half = coarsen(eps_fine)
        eps_quarter = coarsen(eps_half)
        levels = [(eps_fine, diagonal_of(eps_fine, 1.0), 1.0),
                  (eps_half, diagonal_of(eps_half, 0.25), 0.25),
                  (eps_quarter, diagonal_of(eps_quarter, 0.0625), 0.0625)]
        potential = None
        for cycle_index in range(CYCLES):
            potential = multigrid_cycle(0, potential, rhs_fine, levels)
        to_first = potential * moved
        to_second = shift_rows(potential * phi_first, -row_offset)
        summed = summed.at[first_index].add(-to_first)
        summed = summed.at[second_index].add(-to_second)
        return summed

    summed = lax.fori_loop(0, pair_total, one_pair, jnp.zeros(orbital_cubes.shape, jnp.float32))
    return summed.reshape(orbital_count, B, B * B)
```

```python
import functools

import jax
import jax.numpy as jnp
from jax import lax
from jax.experimental import pallas as pl
from jax.experimental.pallas import tpu as pltpu
from jax.sharding import PartitionSpec as P

B = 32
PMAX = 4
SMAX = 8
CYCLES = 2
SWEEPS = 4
FOURPI = 4.0 * 3.141592653589793
OMEGA = 0.8

SECOND = ((1, 4, 4, 5, 4, 5, 4, 5), (2, 3, 2, 3, 3, 6, 6, 7))
PLACE = ((1, 4, 4, 5, 4, 5, 4, 5), (2, 3, 2, 3, 3, 4, 4, 5))
SLOTS = 8
FRONT = 2
PADDED = 13
ROWS = 64
LANES = 128


def as_rows(value):
    count = value.shape[0]
    return value.reshape(count, 8, 8, LANES).transpose(0, 2, 1, 3).reshape(count, ROWS, LANES)


def from_rows(value):
    count = value.shape[0]
    return value.reshape(count, 8, 8, LANES).transpose(0, 2, 1, 3).reshape(count, 8, 8 * LANES)


def lane_of(shape):
    return lax.broadcasted_iota(jnp.int32, shape, len(shape) - 1)


def fill_padded(pad, place, source, index):
    for block in range(8):
        pad[place, FRONT + block] = source[index, 8 * block : 8 * block + 8, :]


def clear_margins(pad, count):
    nothing = jnp.zeros((8, LANES), jnp.float32)
    for place in range(count):
        for block in (0, 1, 10, 11, 12):
            pad[place, block] = nothing


def shifted(pad, place, delta):
    moved = delta + SMAX
    first = moved >> 2
    part = moved & 3
    turn = (LANES - 32 * part) & (LANES - 1)
    keep = lane_of((8, LANES)) < LANES - 32 * part
    rolled = [pltpu.roll(pad[place, first + block], turn, 1) for block in range(9)]
    return [jnp.where(keep, rolled[block], rolled[block + 1]) for block in range(8)]


def gather_fields(core, own_ref, swap_ref, next_ref, pad):
    for index in range(2):
        fill_padded(pad, 2 * core + index, own_ref, index)
        fill_padded(pad, 2 * (1 - core) + index, swap_ref, index)
        fill_padded(pad, 4 + index, next_ref, index)
    clear_margins(pad, 6)


def pre_kernel(table_ref, own_ref, eps_ref, swap_ref, next_ref, out_ref, pad):
    core = table_ref[2 * SLOTS]
    gather_fields(core, own_ref, swap_ref, next_ref, pad)
    for slot in range(SLOTS):
        moved = shifted(pad, table_ref[SLOTS + slot], table_ref[slot])
        for block in range(8):
            first = pad[slot // 2, FRONT + block]
            out_ref[slot // 2, slot % 2, 8 * block : 8 * block + 8, :] = FOURPI * (
                first * moved[block]
            )
    for index in range(2):
        out_ref[2 * core + index, 2] = eps_ref[index]
        out_ref[2 * (1 - core) + index, 2] = swap_ref[2 + index]


def post_kernel(
    table_ref, own_ref, swap_ref, next_ref, pot_ref, own_out, swap_out, next_out, pad, back, acc
):
    core = table_ref[2 * SLOTS]
    gather_fields(core, own_ref, swap_ref, next_ref, pad)
    clear_margins(back, 2)
    nothing = jnp.zeros((ROWS, LANES), jnp.float32)
    for place in range(6):
        acc[place] = nothing
    for slot in range(SLOTS):
        delta = table_ref[slot]
        place = table_ref[SLOTS + slot]
        live = table_ref[2 * SLOTS + 1 + slot] > 0
        moved = shifted(pad, place, delta)
        for block in range(8):
            rows = slice(8 * block, 8 * block + 8)
            value = jnp.where(live, pot_ref[slot // 2, slot % 2, rows, :], 0.0)
            acc[slot // 2, rows, :] = acc[slot // 2, rows, :] - value * moved[block]
            back[slot % 2, FRONT + block] = value * pad[slot // 2, FRONT + block]
        returned = shifted(back, slot % 2, -delta)
        for block in range(8):
            rows = slice(8 * block, 8 * block + 8)
            acc[place, rows, :] = acc[place, rows, :] - returned[block]
    for index in range(2):
        own_out[index] = acc[2 * core + index]
        swap_out[index] = acc[2 * (1 - core) + index]
        next_out[index] = acc[4 + index]


def roll(value, steps, axis):
    size = value.shape[axis]
    return pltpu.roll(value, steps % size, axis)


def exchange_groups(parts):
    lane = lane_of((8, LANES))
    low = lane < 64
    even = (lane & 32) == 0
    halves = [None] * 4
    for index in range(2):
        above, below = parts[index], parts[index + 2]
        crossed = roll(jnp.where(low, below, above), 64, 1)
        halves[index] = jnp.where(low, above, crossed)
        halves[index + 2] = jnp.where(low, crossed, below)
    result = [None] * 4
    for index in (0, 2):
        left, right = halves[index], halves[index + 1]
        result[index] = jnp.where(even, left, roll(right, 32, 1))
        result[index + 1] = jnp.where(even, roll(left, -32, 1), right)
    return result


class Level:
    def __init__(self, depth):
        self.depth = depth
        self.zs = 8 >> depth
        self.ys = 4 >> depth
        self.step = 1 << depth
        lane = lane_of((8, LANES))
        sub = lax.broadcasted_iota(jnp.int32, (8, LANES), 0)
        column = lane & 31
        self.inside = (
            lane < 96,
            lane >= 32,
            sub < 7,
            sub > 0,
            column < 32 - self.step,
            column >= self.step,
        )

    def neighbours(self, get, q, r):
        zs, ys = self.zs, self.ys
        return (
            get(q + 1, r) if q < zs - 1 else roll(get(0, r), -32, 1),
            get(q - 1, r) if q > 0 else roll(get(zs - 1, r), 32, 1),
            get(q, r + 1) if r < ys - 1 else roll(get(q, 0), -1, 0),
            get(q, r - 1) if r > 0 else roll(get(q, ys - 1), 1, 0),
            roll(get(q, r), -self.step, 1),
            roll(get(q, r), self.step, 1),
        )

    def edges(self, q, r):
        return (
            self.inside[0] if q == self.zs - 1 else None,
            self.inside[1] if q == 0 else None,
            self.inside[2] if r == self.ys - 1 else None,
            self.inside[3] if r == 0 else None,
            self.inside[4],
            self.inside[5],
        )

    def coefficients(self, get, q, r):
        centre = get(q, r)
        edges = self.edges(q, r)
        around = [
            value if edge is None else jnp.where(edge, value, 0.0)
            for value, edge in zip(self.neighbours(get, q, r), edges)
        ]
        total = 6.0 * centre + sum(around[1:], around[0])
        scale = OMEGA / total
        couplings = []
        for value, edge in zip(around, edges):
            coupling = (centre + value) * scale
            couplings.append(coupling if edge is None else jnp.where(edge, coupling, 0.0))
        return couplings, total, scale

    def change(self, get, couplings, source, q, r):
        around = self.neighbours(get, q, r)
        terms = [c * v for c, v in zip(couplings, around)]
        pairs = (terms[0] + terms[1]) + (terms[2] + terms[3]) + (terms[4] + terms[5])
        return (source - OMEGA * get(q, r)) + pairs

    def pair_sum(self, value):
        even = (lane_of((8, LANES)) & self.step) == 0
        return value + jnp.where(even, roll(value, -self.step, 1), roll(value, self.step, 1))

    def block_sums(self, get):
        sums = {}
        for q in range(0, self.zs, 2):
            for r in range(0, self.ys, 2):
                four = (get(q, r) + get(q, r + 1)) + (get(q + 1, r) + get(q + 1, r + 1))
                sums[q // 2, r // 2] = self.pair_sum(four)
        return sums

    def cells(self):
        return [(q, r) for q in range(self.zs) for r in range(self.ys)]


def solve_kernel(in_ref, out_ref, eps, couple, total, source, first, second):
    levels = [Level(depth) for depth in range(3)]
    fine, half, quarter = levels

    def at(ref, *lead):
        return lambda q, r: ref[(*lead, q * 4 + r)]

    for q in range(8):
        for field in range(3):
            parts = [in_ref[part, field, pl.ds(q, 8, stride=8), :] for part in range(4)]
            turned = exchange_groups(parts)
            for r in range(4):
                if field == 2:
                    eps[q * 4 + r] = turned[r]
                else:
                    source[field, q * 4 + r] = turned[r]

    get_eps = at(eps)
    for q, r in fine.cells():
        couplings, summed, scale = fine.coefficients(get_eps, q, r)
        for side in range(6):
            couple[side, q * 4 + r] = couplings[side]
        total[q * 4 + r] = summed
        for slot in range(2):
            source[slot, q * 4 + r] = (2.0 * scale) * source[slot, q * 4 + r]

    def coarse_data(level, eps_sums):
        eps_level = {key: 0.125 * value for key, value in eps_sums.items()}
        get = lambda q, r: eps_level[q, r]
        data = {key: level.coefficients(get, *key) for key in level.cells()}
        return get, data

    get_half, half_data = coarse_data(half, fine.block_sums(get_eps))
    _, quarter_data = coarse_data(quarter, half.block_sums(get_half))

    def smooth(level, data, values, rhs):
        get = lambda q, r: values[q, r]
        return {
            key: level.change(get, data[key][0], rhs[key], *key) for key in level.cells()
        }

    def added(values, changes):
        return {key: values[key] + changes[key] for key in values}

    def restricted(level, data, changes, below, below_data):
        weighted = lambda q, r: data[q, r][1] * changes[q, r]
        sums = level.block_sums(weighted)
        return {key: (0.625 * below_data[key][2]) * sums[key] for key in below.cells()}

    def correction(rhs_half):
        values = rhs_half
        changes = smooth(half, half_data, values, rhs_half)
        rhs_quarter = restricted(half, half_data, changes, quarter, quarter_data)
        lowest = rhs_quarter
        for _ in range(SWEEPS - 1):
            lowest = added(lowest, smooth(quarter, quarter_data, lowest, rhs_quarter))
        values = {(q, r): values[q, r] + lowest[q // 2, r // 2] for q, r in half.cells()}
        return added(values, smooth(half, half_data, values, rhs_half))

    def fine_change(ref, slot, q, r):
        couplings = [couple[side, q * 4 + r] for side in range(6)]
        return fine.change(at(ref, slot), couplings, source[slot, q * 4 + r], q, r)

    def coarse_rhs(ref):
        result = [{}, {}]
        for q in range(0, 8, 2):
            for r in range(0, 4, 2):
                for slot in range(2):
                    four = None
                    for qq, rr in ((q, r), (q, r + 1), (q + 1, r), (q + 1, r + 1)):
                        term = total[qq * 4 + rr] * fine_change(ref, slot, qq, rr)
                        four = term if four is None else four + term
                    key = (q // 2, r // 2)
                    result[slot][key] = (0.625 * half_data[key][2]) * fine.pair_sum(four)
        return result

    def relax(ref, target):
        for q, r in fine.cells():
            for slot in range(2):
                target(slot, q, r, ref[slot, q * 4 + r] + fine_change(ref, slot, q, r))

    def into(ref):
        def put(slot, q, r, value):
            ref[slot, q * 4 + r] = value

        return put

    def corrected(ref, target):
        rhs = coarse_rhs(ref)
        extra = [correction(rhs[slot]) for slot in range(2)]
        for q, r in fine.cells():
            for slot in range(2):
                target[slot, q * 4 + r] = ref[slot, q * 4 + r] + extra[slot][q // 2, r // 2]

    corrected(source, first)
    for _ in range(CYCLES - 1):
        relax(first, into(second))
        relax(second, into(first))
        corrected(first, first)
    relax(first, into(second))
    for q in range(8):
        for slot in range(2):
            turned = exchange_groups([second[slot, q * 4 + r] for r in range(4)])
            for part in range(4):
                out_ref[part, slot, pl.ds(q, 8, stride=8), :] = turned[part]


def near(value):
    return pltpu.with_memory_space_constraint(value, pltpu.VMEM)


def slot_table(owner, pair_offsets, pair_counts, box_shift):
    core = owner % 2
    base = 2 * (owner - core)
    first = jnp.repeat(jnp.arange(PMAX, dtype=jnp.int32), 2)
    second = jnp.where(core == 0, jnp.array(SECOND[0], jnp.int32), jnp.array(SECOND[1], jnp.int32))
    place = jnp.where(core == 0, jnp.array(PLACE[0], jnp.int32), jnp.array(PLACE[1], jnp.int32))
    counts = lax.dynamic_slice(pair_counts, (base,), (4,))
    offsets = lax.dynamic_slice(pair_offsets, (base, 0), (4, PMAX))
    looped = jnp.concatenate([box_shift, box_shift[:4]])
    shifts = lax.dynamic_slice(looped, (base,), (8,))
    named = jnp.arange(8, dtype=jnp.int32)[None, :] == second[:, None]
    delta = jnp.repeat(shifts[:4], 2) - jnp.sum(jnp.where(named, shifts[None, :], 0), axis=1)
    listed = jnp.arange(PMAX, dtype=jnp.int32)[None, :] < jnp.repeat(counts, 2)[:, None]
    wanted = jnp.repeat(offsets, 2, axis=0) + 1 == (second - first)[:, None]
    live = jnp.any(listed & wanted, axis=1).astype(jnp.int32)
    return jnp.concatenate([delta, place, core[None].astype(jnp.int32), live])


def shards(orbitals, dielectric, pair_offsets, pair_counts, box_shift):
    owner = lax.axis_index("orb")
    owners = lax.axis_size("orb")
    swapped = [(source, source ^ 1) for source in range(owners)]
    back_chip = [(source, (source - 2) % owners) for source in range(owners)]
    next_chip = [(source, (source + 2) % owners) for source in range(owners)]

    own = as_rows(orbitals)
    eps = as_rows(dielectric)
    beyond = lax.ppermute(own, "orb", back_chip)
    across = lax.ppermute(jnp.concatenate([own, eps]), "orb", swapped)
    table = slot_table(owner, pair_offsets, pair_counts, box_shift)

    smem = pl.BlockSpec(memory_space=pltpu.SMEM)
    vmem = pl.BlockSpec(memory_space=pltpu.VMEM)
    pad_scratch = pltpu.VMEM((6, PADDED, 8, LANES), jnp.float32)
    requests = pl.pallas_call(
        pre_kernel,
        out_shape=pltpu.VMEM((4, 3, ROWS, LANES), jnp.float32),
        in_specs=[smem, vmem, vmem, vmem, vmem],
        out_specs=vmem,
        scratch_shapes=[pad_scratch],
        name="pair_sources",
    )(table, near(own), near(eps), near(across), near(beyond))
    arrived = lax.all_to_all(requests, "grid", 0, 0)
    cells = (32, 8, LANES)
    potentials = pl.pallas_call(
        solve_kernel,
        out_shape=pltpu.VMEM((4, 2, ROWS, LANES), jnp.float32),
        in_specs=[vmem],
        out_specs=vmem,
        scratch_shapes=[
            pltpu.VMEM(cells, jnp.float32),
            pltpu.VMEM((6, *cells), jnp.float32),
            pltpu.VMEM(cells, jnp.float32),
            pltpu.VMEM((2, *cells), jnp.float32),
            pltpu.VMEM((2, *cells), jnp.float32),
            pltpu.VMEM((2, *cells), jnp.float32),
        ],
        name="pair_solve",
    )(near(arrived))
    returned = lax.all_to_all(potentials, "grid", 0, 0)
    two = pltpu.VMEM((2, ROWS, LANES), jnp.float32)
    mine, theirs, later = pl.pallas_call(
        post_kernel,
        out_shape=(two, two, two),
        in_specs=[smem, vmem, vmem, vmem, vmem],
        out_specs=(vmem, vmem, vmem),
        scratch_shapes=[
            pad_scratch,
            pltpu.VMEM((2, PADDED, 8, LANES), jnp.float32),
            pltpu.VMEM((6, ROWS, LANES), jnp.float32),
        ],
        name="pair_actions",
    )(table, near(own), near(across), near(beyond), near(returned))
    from_chip = lax.ppermute(theirs, "orb", swapped)
    from_before = lax.ppermute(later, "orb", next_chip)
    return from_rows(mine + from_chip + from_before)


def solution(mesh):
    placed = (P("orb", "grid", None), P("orb", "grid", None), P(), P(), P())
    return jax.shard_map(
        shards, mesh=mesh, in_specs=placed, out_specs=P("orb", "grid", None), check_vma=False
    )
```

```python
import jax
import jax.numpy as jnp
from jax import lax
from jax.experimental import pallas as pl
from jax.experimental.pallas import tpu as pltpu
from jax.sharding import PartitionSpec as P

PMAX = 4
SMAX = 8
CYCLES = 2
SWEEPS = 4
FOURPI = 4.0 * 3.141592653589793
OMEGA = 0.8

SECOND = ((1, 4, 4, 5, 4, 5, 4, 5), (2, 3, 2, 3, 3, 6, 6, 7))
PLACE = ((1, 4, 4, 5, 4, 5, 4, 5), (2, 3, 2, 3, 3, 4, 4, 5))
SLOTS = 8
FRONT = 2
PADDED = 13
ROWS = 64
LANES = 128


def as_rows(value):
    count = value.shape[0]
    return value.reshape(count, 8, 8, LANES).transpose(0, 2, 1, 3).reshape(count, ROWS, LANES)


def from_rows(value):
    count = value.shape[0]
    return value.reshape(count, 8, 8, LANES).transpose(0, 2, 1, 3).reshape(count, 8, 8 * LANES)


def lane_of(shape):
    return lax.broadcasted_iota(jnp.int32, shape, len(shape) - 1)


def fill_padded(pad, place, source, index):
    for block in range(8):
        pad[place, FRONT + block] = source[index, 8 * block : 8 * block + 8, :]


def clear_margins(pad, count):
    nothing = jnp.zeros((8, LANES), jnp.float32)
    for place in range(count):
        for block in (0, 1, 10, 11, 12):
            pad[place, block] = nothing


def shifted(pad, place, delta):
    moved = delta + SMAX
    first = moved >> 2
    part = moved & 3
    turn = (LANES - 32 * part) & (LANES - 1)
    keep = lane_of((8, LANES)) < LANES - 32 * part
    rolled = [pltpu.roll(pad[place, first + block], turn, 1) for block in range(9)]
    return [jnp.where(keep, rolled[block], rolled[block + 1]) for block in range(8)]


def gather_fields(core, own_ref, swap_ref, next_ref, pad):
    for index in range(2):
        fill_padded(pad, 2 * core + index, own_ref, index)
        fill_padded(pad, 2 * (1 - core) + index, swap_ref, index)
        fill_padded(pad, 4 + index, next_ref, index)
    clear_margins(pad, 6)


def pre_kernel(table_ref, own_ref, swap_ref, next_ref, out_ref, pad):
    core = table_ref[2 * SLOTS]
    gather_fields(core, own_ref, swap_ref, next_ref, pad)
    for slot in range(SLOTS):
        moved = shifted(pad, table_ref[SLOTS + slot], table_ref[slot])
        for block in range(8):
            first = pad[slot // 2, FRONT + block]
            out_ref[slot // 2, slot % 2, 8 * block : 8 * block + 8, :] = FOURPI * (
                first * moved[block]
            )
    for index in range(2):
        out_ref[2 * core + index, 2] = own_ref[2 + index]
        out_ref[2 * (1 - core) + index, 2] = swap_ref[2 + index]


def post_kernel(
    table_ref, own_ref, swap_ref, next_ref, pot_ref, own_out, swap_out, next_out, pad, back, acc
):
    core = table_ref[2 * SLOTS]
    gather_fields(core, own_ref, swap_ref, next_ref, pad)
    clear_margins(back, 2)
    nothing = jnp.zeros((ROWS, LANES), jnp.float32)
    for place in range(6):
        acc[place] = nothing
    for slot in range(SLOTS):
        delta = table_ref[slot]
        place = table_ref[SLOTS + slot]
        live = table_ref[2 * SLOTS + 1 + slot] > 0
        moved = shifted(pad, place, delta)
        for block in range(8):
            rows = slice(8 * block, 8 * block + 8)
            value = jnp.where(live, pot_ref[slot // 2, slot % 2, rows, :], 0.0)
            acc[slot // 2, rows, :] = acc[slot // 2, rows, :] - value * moved[block]
            back[slot % 2, FRONT + block] = value * pad[slot // 2, FRONT + block]
        returned = shifted(back, slot % 2, -delta)
        for block in range(8):
            rows = slice(8 * block, 8 * block + 8)
            acc[place, rows, :] = acc[place, rows, :] - returned[block]
    for index in range(2):
        own_out[index] = acc[2 * core + index]
        swap_out[index] = acc[2 * (1 - core) + index]
        next_out[index] = acc[4 + index]


def roll(value, steps, axis):
    size = value.shape[axis]
    return pltpu.roll(value, steps % size, axis)


def exchange_groups(parts):
    lane = lane_of((8, LANES))
    low = lane < 64
    even = (lane & 32) == 0
    halves = [None] * 4
    for index in range(2):
        above, below = parts[index], parts[index + 2]
        crossed = roll(jnp.where(low, below, above), 64, 1)
        halves[index] = jnp.where(low, above, crossed)
        halves[index + 2] = jnp.where(low, crossed, below)
    result = [None] * 4
    for index in (0, 2):
        left, right = halves[index], halves[index + 1]
        result[index] = jnp.where(even, left, roll(right, 32, 1))
        result[index + 1] = jnp.where(even, roll(left, -32, 1), right)
    return result


class Level:
    def __init__(self, depth):
        self.zs = 8 >> depth
        self.ys = 4 >> depth
        self.step = 1 << depth
        lane = lane_of((8, LANES))
        sub = lax.broadcasted_iota(jnp.int32, (8, LANES), 0)
        column = lane & 31
        self.inside = (
            lane < 96,
            lane >= 32,
            sub < 7,
            sub > 0,
            column < 32 - self.step,
            column >= self.step,
        )

    def neighbours(self, get, q, r):
        ys = self.ys
        return (
            get(q + 1, r),
            get(q - 1, r),
            get(q, r + 1) if r < ys - 1 else roll(get(q, 0), -1, 0),
            get(q, r - 1) if r > 0 else roll(get(q, ys - 1), 1, 0),
            roll(get(q, r), -self.step, 1),
            roll(get(q, r), self.step, 1),
        )

    def wrapped(self, values):
        zs = self.zs

        def get(q, r):
            if q == zs:
                return roll(values[0, r], -32, 1)
            if q == -1:
                return roll(values[zs - 1, r], 32, 1)
            return values[q, r]

        return get

    def edges(self, q, r):
        return (
            self.inside[0] if q == self.zs - 1 else None,
            self.inside[1] if q == 0 else None,
            self.inside[2] if r == self.ys - 1 else None,
            self.inside[3] if r == 0 else None,
            self.inside[4],
            self.inside[5],
        )

    def coefficients(self, get, q, r):
        centre = get(q, r)
        edges = self.edges(q, r)
        around = [
            value if edge is None else jnp.where(edge, value, 0.0)
            for value, edge in zip(self.neighbours(get, q, r), edges)
        ]
        total = 6.0 * centre + sum(around[1:], around[0])
        scale = OMEGA / total
        couplings = []
        for value, edge in zip(around, edges):
            coupling = (centre + value) * scale
            couplings.append(coupling if edge is None else jnp.where(edge, coupling, 0.0))
        return couplings, total, scale

    def coupled(self, get, couplings, q, r):
        terms = [c * v for c, v in zip(couplings, self.neighbours(get, q, r))]
        return (terms[0] + terms[1]) + (terms[2] + terms[3]) + (terms[4] + terms[5])

    def pair_sum(self, value):
        even = (lane_of((8, LANES)) & self.step) == 0
        return value + jnp.where(even, roll(value, -self.step, 1), roll(value, self.step, 1))

    def block_sums(self, get):
        sums = {}
        for q in range(0, self.zs, 2):
            for r in range(0, self.ys, 2):
                four = (get(q, r) + get(q, r + 1)) + (get(q + 1, r) + get(q + 1, r + 1))
                sums[q // 2, r // 2] = self.pair_sum(four)
        return sums

    def cells(self):
        return [(q, r) for q in range(self.zs) for r in range(self.ys)]


def solve_kernel(in_ref, out_ref, eps, couple, total, source, field, half_ref, quarter_ref):
    fine, half, quarter = Level(0), Level(1), Level(2)
    slots = (0, 1)

    def place(q, r):
        return (q + 1) * 4 + r

    def at(ref, *lead):
        return lambda q, r: ref[(*lead, place(q, r))]

    def close_ends(ref, *lead):
        for r in range(4):
            ref[(*lead, place(8, r))] = roll(ref[(*lead, place(0, r))], -32, 1)
            ref[(*lead, place(-1, r))] = roll(ref[(*lead, place(7, r))], 32, 1)

    for q in range(8):
        for which in range(3):
            parts = [in_ref[part, which, pl.ds(q, 8, stride=8), :] for part in range(4)]
            turned = exchange_groups(parts)
            for r in range(4):
                if which == 2:
                    eps[place(q, r)] = turned[r]
                else:
                    source[which, q * 4 + r] = turned[r]
    close_ends(eps)

    get_eps = at(eps)
    for q, r in fine.cells():
        couplings, summed, scale = fine.coefficients(get_eps, q, r)
        for side in range(6):
            couple[side, q * 4 + r] = couplings[side]
        total[q * 4 + r] = summed
        for slot in slots:
            started = (2.0 * scale) * source[slot, q * 4 + r]
            source[slot, q * 4 + r] = started
            field[0, slot, place(q, r)] = started
    for slot in slots:
        close_ends(field, 0, slot)

    def keep_level(level, ref, eps_level):
        get = level.wrapped(eps_level)
        for q, r in level.cells():
            couplings, summed, scale = level.coefficients(get, q, r)
            for side in range(6):
                ref[side, q * level.ys + r] = couplings[side]
            ref[6, q * level.ys + r] = summed
            ref[7, q * level.ys + r] = 0.625 * scale

    def means(level, get):
        return {key: 0.125 * value for key, value in level.block_sums(get).items()}

    eps_half = means(fine, get_eps)
    keep_level(half, half_ref, eps_half)
    keep_level(quarter, quarter_ref, means(half, lambda q, r: eps_half[q, r]))

    def kept(level, ref, item, q, r):
        return ref[item, q * level.ys + r]

    def around(level, ref, values, q, r):
        couplings = [kept(level, ref, side, q, r) for side in range(6)]
        return level.coupled(level.wrapped(values), couplings, q, r)

    def relaxed(level, ref, values, rhs):
        return {
            (q, r): ((1.0 - OMEGA) * values[q, r] + rhs[q, r]) + around(level, ref, values, q, r)
            for q, r in level.cells()
        }

    def correction(rhs):
        def weighted(q, r):
            return kept(half, half_ref, 6, q, r) * (
                (1.0 - OMEGA) * rhs[q, r] + around(half, half_ref, rhs, q, r)
            )

        sums = half.block_sums(weighted)
        start = {key: kept(quarter, quarter_ref, 7, *key) * sums[key] for key in quarter.cells()}
        lowest = start
        for _ in range(SWEEPS - 1):
            lowest = relaxed(quarter, quarter_ref, lowest, start)
        values = {(q, r): rhs[q, r] + lowest[q // 2, r // 2] for q, r in half.cells()}
        return relaxed(half, half_ref, values, rhs)

    def fine_coupled(couplings, lead, q, r):
        return fine.coupled(at(field, *lead), couplings, q, r)

    def fine_couplings(q, r):
        return [couple[side, q * 4 + r] for side in range(6)]

    def correct():
        rhs = ({}, {})
        for q in range(0, 8, 2):
            for r in range(0, 4, 2):
                four = [None, None]
                for qq, rr in ((q, r), (q, r + 1), (q + 1, r), (q + 1, r + 1)):
                    couplings = fine_couplings(qq, rr)
                    for slot in slots:
                        left = source[slot, qq * 4 + rr] - OMEGA * field[0, slot, place(qq, rr)]
                        left = left + fine_coupled(couplings, (0, slot), qq, rr)
                        term = total[qq * 4 + rr] * left
                        four[slot] = term if four[slot] is None else four[slot] + term
                key = (q // 2, r // 2)
                for slot in slots:
                    rhs[slot][key] = kept(half, half_ref, 7, *key) * fine.pair_sum(four[slot])
        extra = [correction(rhs[slot]) for slot in slots]
        for slot in slots:
            for q, r in fine.cells():
                corrected = field[0, slot, place(q, r)] + extra[slot][q // 2, r // 2]
                field[0, slot, place(q, r)] = corrected
            close_ends(field, 0, slot)

    def relax(before, after):
        for q, r in fine.cells():
            couplings = fine_couplings(q, r)
            for slot in slots:
                value = (1.0 - OMEGA) * field[before, slot, place(q, r)]
                value = value + source[slot, q * 4 + r]
                value = value + fine_coupled(couplings, (before, slot), q, r)
                field[after, slot, place(q, r)] = value
        for slot in slots:
            close_ends(field, after, slot)

    def cycle(index, carry):
        correct()
        relax(0, 1)

        @pl.when(index < CYCLES - 1)
        def _():
            relax(1, 0)

        return carry

    lax.fori_loop(0, CYCLES, cycle, 0)
    for q in range(8):
        for slot in slots:
            turned = exchange_groups([field[1, slot, place(q, r)] for r in range(4)])
            for part in range(4):
                out_ref[part, slot, pl.ds(q, 8, stride=8), :] = turned[part]


def near(value):
    return pltpu.with_memory_space_constraint(value, pltpu.VMEM)


def in_scalars(value):
    return pltpu.with_memory_space_constraint(value, pltpu.SMEM)


def fill_table(owner, offsets_ref, counts_ref, shift_ref, table_ref):
    core = owner & 1
    base = 2 * (owner - core)
    orbital_count = counts_ref.shape[0]
    for slot in range(SLOTS):
        first = slot // 2
        second = jnp.where(core == 0, SECOND[0][slot], SECOND[1][slot])
        other = base + second
        other = jnp.where(other >= orbital_count, other - orbital_count, other)
        table_ref[slot] = shift_ref[base + first] - shift_ref[other]
        table_ref[SLOTS + slot] = jnp.where(core == 0, PLACE[0][slot], PLACE[1][slot])
        count = counts_ref[base + first]
        live = jnp.int32(0)
        for rank in range(PMAX):
            listed = (count > rank) & (offsets_ref[rank, base + first] + 1 == second - first)
            live = live + listed.astype(jnp.int32)
        table_ref[2 * SLOTS + 1 + slot] = live
    table_ref[2 * SLOTS] = core


def prepare_kernel(
    own_hbm, eps_hbm, offsets_hbm, counts_hbm, shift_hbm,
    packet_ref, table_ref,
    offsets_ref, counts_ref, shift_ref, sems,
):
    copies = [
        pltpu.make_async_copy(offsets_hbm, offsets_ref, sems.at[0]),
        pltpu.make_async_copy(counts_hbm, counts_ref, sems.at[1]),
        pltpu.make_async_copy(shift_hbm, shift_ref, sems.at[2]),
        pltpu.make_async_copy(own_hbm, packet_ref.at[0:2], sems.at[3]),
        pltpu.make_async_copy(eps_hbm, packet_ref.at[2:4], sems.at[4]),
    ]
    for copy in copies:
        copy.start()
    for copy in copies[:3]:
        copy.wait()
    fill_table(lax.axis_index("orb"), offsets_ref, counts_ref, shift_ref, table_ref)
    for copy in copies[3:]:
        copy.wait()


def shards(orbitals, dielectric, pair_offsets, pair_counts, box_shift):
    owners = lax.axis_size("orb")
    swapped = [(source, source ^ 1) for source in range(owners)]
    back_chip = [(source, (source - 2) % owners) for source in range(owners)]
    next_chip = [(source, (source + 2) % owners) for source in range(owners)]

    own = as_rows(orbitals)
    eps = as_rows(dielectric)
    beyond = lax.ppermute(own, "orb", back_chip)
    smem = pl.BlockSpec(memory_space=pltpu.SMEM)
    vmem = pl.BlockSpec(memory_space=pltpu.VMEM)
    anywhere = pl.BlockSpec(memory_space=pl.ANY)
    count = pair_counts.shape[0]
    packet, table = pl.pallas_call(
        prepare_kernel,
        out_shape=(
            pltpu.VMEM((4, ROWS, LANES), jnp.float32),
            pltpu.SMEM((3 * SLOTS + 1,), jnp.int32),
        ),
        in_specs=[anywhere] * 5,
        out_specs=(vmem, smem),
        scratch_shapes=[
            pltpu.SMEM((PMAX, count), jnp.int32),
            pltpu.SMEM((count,), jnp.int32),
            pltpu.SMEM((count,), jnp.int32),
            pltpu.SemaphoreType.DMA((5,)),
        ],
        name="pair_prepare",
    )(own, eps, pair_offsets.T, pair_counts, box_shift)
    table = in_scalars(table)
    across = lax.ppermute(packet, "orb", swapped)
    pad_scratch = pltpu.VMEM((6, PADDED, 8, LANES), jnp.float32)
    requests = pl.pallas_call(
        pre_kernel,
        out_shape=pltpu.VMEM((4, 3, ROWS, LANES), jnp.float32),
        in_specs=[smem, vmem, vmem, vmem],
        out_specs=vmem,
        scratch_shapes=[pad_scratch],
        name="pair_sources",
    )(table, near(packet), near(across), near(beyond))
    arrived = lax.all_to_all(requests, "grid", 0, 0)
    cells = (32, 8, LANES)
    ended = (40, 8, LANES)
    potentials = pl.pallas_call(
        solve_kernel,
        out_shape=pltpu.VMEM((4, 2, ROWS, LANES), jnp.float32),
        in_specs=[vmem],
        out_specs=vmem,
        scratch_shapes=[
            pltpu.VMEM(ended, jnp.float32),
            pltpu.VMEM((6, *cells), jnp.float32),
            pltpu.VMEM(cells, jnp.float32),
            pltpu.VMEM((2, *cells), jnp.float32),
            pltpu.VMEM((2, 2, *ended), jnp.float32),
            pltpu.VMEM((8, 8, 8, LANES), jnp.float32),
            pltpu.VMEM((8, 2, 8, LANES), jnp.float32),
        ],
        name="pair_solve",
    )(near(arrived))
    returned = lax.all_to_all(potentials, "grid", 0, 0)
    two = pltpu.VMEM((2, ROWS, LANES), jnp.float32)
    mine, theirs, later = pl.pallas_call(
        post_kernel,
        out_shape=(two, two, two),
        in_specs=[smem, vmem, vmem, vmem, vmem],
        out_specs=(vmem, vmem, vmem),
        scratch_shapes=[
            pad_scratch,
            pltpu.VMEM((2, PADDED, 8, LANES), jnp.float32),
            pltpu.VMEM((6, ROWS, LANES), jnp.float32),
        ],
        name="pair_actions",
    )(table, near(packet), near(across), near(beyond), near(returned))
    from_before = lax.ppermute(later, "orb", next_chip)
    from_chip = lax.ppermute(theirs, "orb", swapped)
    return from_rows(mine + from_chip + from_before)


def solution(mesh):
    placed = (P("orb", "grid", None), P("orb", "grid", None), P(), P(), P())
    return jax.shard_map(
        shards, mesh=mesh, in_specs=placed, out_specs=P("orb", "grid", None), check_vma=False
    )
```

```python
import jax
import jax.numpy as jnp
from jax import lax
from jax.experimental import pallas as pl
from jax.experimental.pallas import tpu as pltpu
from jax.sharding import PartitionSpec as P

PMAX = 4
SMAX = 8
CYCLES = 2
SWEEPS = 4
FOURPI = 4.0 * 3.141592653589793
OMEGA = 0.8

SLOTS = 8
ONE = ((0, 0, 1, 1, 2, 2, 3, 3), (0, 0, 0, 0, 1, 1, 1, 1))
OTHER = ((1, 2, 2, 3, 4, 5, 4, 5), (1, 2, 3, 4, 2, 3, 4, 5))
DELTA, FIRST, SECOND, LIVE, CORE = 0, SLOTS, 2 * SLOTS, 3 * SLOTS, 4 * SLOTS
FRONT = 2
PADDED = 13
ROWS = 64
LANES = 128


def as_rows(value):
    count = value.shape[0]
    return value.reshape(count, 8, 8, LANES).transpose(0, 2, 1, 3).reshape(count, ROWS, LANES)


def from_rows(value):
    count = value.shape[0]
    return value.reshape(count, 8, 8, LANES).transpose(0, 2, 1, 3).reshape(count, 8, 8 * LANES)


def lane_of(shape):
    return lax.broadcasted_iota(jnp.int32, shape, len(shape) - 1)


def fill_padded(pad, place, source, index):
    for block in range(8):
        pad[place, FRONT + block] = source[index, 8 * block : 8 * block + 8, :]


def clear_margins(pad, count):
    nothing = jnp.zeros((8, LANES), jnp.float32)
    for place in range(count):
        for block in (0, 1, 10, 11, 12):
            pad[place, block] = nothing


def shifted(pad, place, delta):
    moved = delta + SMAX
    first = moved >> 2
    part = moved & 3
    turn = (LANES - 32 * part) & (LANES - 1)
    keep = lane_of((8, LANES)) < LANES - 32 * part
    rolled = [pltpu.roll(pad[place, first + block], turn, 1) for block in range(9)]
    return [jnp.where(keep, rolled[block], rolled[block + 1]) for block in range(8)]


def gather_fields(core, before_ref, across_ref, own_ref, pad):
    for index in range(2):
        fill_padded(pad, index, before_ref, index)
        fill_padded(pad, 2 + 2 * core + index, own_ref, index)
        fill_padded(pad, 4 - 2 * core + index, across_ref, index)
    clear_margins(pad, 6)


def pre_kernel(table_ref, before_ref, across_ref, own_ref, out_ref, pad):
    core = table_ref[CORE]
    gather_fields(core, before_ref, across_ref, own_ref, pad)
    for slot in range(SLOTS):
        one, other = table_ref[FIRST + slot], table_ref[SECOND + slot]
        moved = shifted(pad, other, table_ref[DELTA + slot])
        for block in range(8):
            out_ref[slot // 2, slot % 2, 8 * block : 8 * block + 8, :] = FOURPI * (
                pad[one, FRONT + block] * moved[block]
            )
    out_ref[0, 2] = before_ref[2]
    out_ref[1, 2] = before_ref[3 - core]
    out_ref[2, 2] = jnp.where(core == 0, own_ref[2], before_ref[3])
    out_ref[3, 2] = jnp.where(core == 0, own_ref[3], before_ref[3])


def post_kernel(
    table_ref, before_ref, across_ref, own_ref, pot_ref, before_out, across_out, own_out, pad, back, acc
):
    core = table_ref[CORE]
    gather_fields(core, before_ref, across_ref, own_ref, pad)
    clear_margins(back, 2)
    nothing = jnp.zeros((ROWS, LANES), jnp.float32)
    for place in range(6):
        acc[place] = nothing
    for slot in range(SLOTS):
        delta = table_ref[DELTA + slot]
        one, other = table_ref[FIRST + slot], table_ref[SECOND + slot]
        live = table_ref[LIVE + slot] > 0
        moved = shifted(pad, other, delta)
        for block in range(8):
            rows = slice(8 * block, 8 * block + 8)
            value = jnp.where(live, pot_ref[slot // 2, slot % 2, rows, :], 0.0)
            acc[one, rows, :] = acc[one, rows, :] - value * moved[block]
            back[slot % 2, FRONT + block] = value * pad[one, FRONT + block]
        returned = shifted(back, slot % 2, -delta)
        for block in range(8):
            rows = slice(8 * block, 8 * block + 8)
            acc[other, rows, :] = acc[other, rows, :] - returned[block]
    for index in range(2):
        before_out[index] = acc[index]
        own_out[index] = acc[2 + 2 * core + index]
        across_out[index] = acc[4 - 2 * core + index]


def roll(value, steps, axis):
    size = value.shape[axis]
    return pltpu.roll(value, steps % size, axis)


def exchange_groups(parts):
    lane = lane_of((8, LANES))
    low = lane < 64
    even = (lane & 32) == 0
    halves = [None] * 4
    for index in range(2):
        above, below = parts[index], parts[index + 2]
        crossed = roll(jnp.where(low, below, above), 64, 1)
        halves[index] = jnp.where(low, above, crossed)
        halves[index + 2] = jnp.where(low, crossed, below)
    result = [None] * 4
    for index in (0, 2):
        left, right = halves[index], halves[index + 1]
        result[index] = jnp.where(even, left, roll(right, 32, 1))
        result[index + 1] = jnp.where(even, roll(left, -32, 1), right)
    return result


class Level:
    def __init__(self, depth):
        self.zs = 8 >> depth
        self.ys = 4 >> depth
        self.step = 1 << depth
        lane = lane_of((8, LANES))
        sub = lax.broadcasted_iota(jnp.int32, (8, LANES), 0)
        column = lane & 31
        self.inside = (
            lane < 96,
            lane >= 32,
            sub < 7,
            sub > 0,
            column < 32 - self.step,
            column >= self.step,
        )

    def neighbours(self, get, q, r):
        ys = self.ys
        return (
            get(q + 1, r),
            get(q - 1, r),
            get(q, r + 1) if r < ys - 1 else roll(get(q, 0), -1, 0),
            get(q, r - 1) if r > 0 else roll(get(q, ys - 1), 1, 0),
            roll(get(q, r), -self.step, 1),
            roll(get(q, r), self.step, 1),
        )

    def wrapped(self, values):
        zs = self.zs

        def get(q, r):
            if q == zs:
                return roll(values[0, r], -32, 1)
            if q == -1:
                return roll(values[zs - 1, r], 32, 1)
            return values[q, r]

        return get

    def edges(self, q, r):
        return (
            self.inside[0] if q == self.zs - 1 else None,
            self.inside[1] if q == 0 else None,
            self.inside[2] if r == self.ys - 1 else None,
            self.inside[3] if r == 0 else None,
            self.inside[4],
            self.inside[5],
        )

    def coefficients(self, get, q, r):
        centre = get(q, r)
        edges = self.edges(q, r)
        around = [
            value if edge is None else jnp.where(edge, value, 0.0)
            for value, edge in zip(self.neighbours(get, q, r), edges)
        ]
        total = 6.0 * centre + sum(around[1:], around[0])
        scale = OMEGA / total
        couplings = []
        for value, edge in zip(around, edges):
            coupling = (centre + value) * scale
            couplings.append(coupling if edge is None else jnp.where(edge, coupling, 0.0))
        return couplings, total, scale

    def coupled(self, get, couplings, q, r):
        terms = [c * v for c, v in zip(couplings, self.neighbours(get, q, r))]
        return (terms[0] + terms[1]) + (terms[2] + terms[3]) + (terms[4] + terms[5])

    def pair_sum(self, value):
        even = (lane_of((8, LANES)) & self.step) == 0
        return value + jnp.where(even, roll(value, -self.step, 1), roll(value, self.step, 1))

    def block_sums(self, get):
        sums = {}
        for q in range(0, self.zs, 2):
            for r in range(0, self.ys, 2):
                four = (get(q, r) + get(q, r + 1)) + (get(q + 1, r) + get(q + 1, r + 1))
                sums[q // 2, r // 2] = self.pair_sum(four)
        return sums

    def cells(self):
        return [(q, r) for q in range(self.zs) for r in range(self.ys)]


def solve_kernel(in_ref, out_ref, eps, couple, total, source, field, half_ref, quarter_ref):
    fine, half, quarter = Level(0), Level(1), Level(2)
    slots = (0, 1)

    def place(q, r):
        return (q + 1) * 4 + r

    def at(ref, *lead):
        return lambda q, r: ref[(*lead, place(q, r))]

    def close_ends(ref, *lead):
        for r in range(4):
            ref[(*lead, place(8, r))] = roll(ref[(*lead, place(0, r))], -32, 1)
            ref[(*lead, place(-1, r))] = roll(ref[(*lead, place(7, r))], 32, 1)

    for q in range(8):
        for which in range(3):
            parts = [in_ref[part, which, pl.ds(q, 8, stride=8), :] for part in range(4)]
            turned = exchange_groups(parts)
            for r in range(4):
                if which == 2:
                    eps[place(q, r)] = turned[r]
                else:
                    source[which, q * 4 + r] = turned[r]
    close_ends(eps)

    get_eps = at(eps)
    for q, r in fine.cells():
        couplings, summed, scale = fine.coefficients(get_eps, q, r)
        for side in range(6):
            couple[side, q * 4 + r] = couplings[side]
        total[q * 4 + r] = summed
        for slot in slots:
            started = (2.0 * scale) * source[slot, q * 4 + r]
            source[slot, q * 4 + r] = started
            field[0, slot, place(q, r)] = started
    for slot in slots:
        close_ends(field, 0, slot)

    def keep_level(level, ref, eps_level):
        get = level.wrapped(eps_level)
        for q, r in level.cells():
            couplings, summed, scale = level.coefficients(get, q, r)
            for side in range(6):
                ref[side, q * level.ys + r] = couplings[side]
            ref[6, q * level.ys + r] = summed
            ref[7, q * level.ys + r] = 0.625 * scale

    def means(level, get):
        return {key: 0.125 * value for key, value in level.block_sums(get).items()}

    eps_half = means(fine, get_eps)
    keep_level(half, half_ref, eps_half)
    keep_level(quarter, quarter_ref, means(half, lambda q, r: eps_half[q, r]))

    def kept(level, ref, item, q, r):
        return ref[item, q * level.ys + r]

    def around(level, ref, values, q, r):
        couplings = [kept(level, ref, side, q, r) for side in range(6)]
        return level.coupled(level.wrapped(values), couplings, q, r)

    def relaxed(level, ref, values, rhs):
        return {
            (q, r): ((1.0 - OMEGA) * values[q, r] + rhs[q, r]) + around(level, ref, values, q, r)
            for q, r in level.cells()
        }

    def correction(rhs):
        def weighted(q, r):
            return kept(half, half_ref, 6, q, r) * (
                (1.0 - OMEGA) * rhs[q, r] + around(half, half_ref, rhs, q, r)
            )

        sums = half.block_sums(weighted)
        start = {key: kept(quarter, quarter_ref, 7, *key) * sums[key] for key in quarter.cells()}
        lowest = start
        for _ in range(SWEEPS - 1):
            lowest = relaxed(quarter, quarter_ref, lowest, start)
        values = {(q, r): rhs[q, r] + lowest[q // 2, r // 2] for q, r in half.cells()}
        return relaxed(half, half_ref, values, rhs)

    def fine_coupled(couplings, lead, q, r):
        return fine.coupled(at(field, *lead), couplings, q, r)

    def fine_couplings(q, r):
        return [couple[side, q * 4 + r] for side in range(6)]

    def correct():
        rhs = ({}, {})
        for q in range(0, 8, 2):
            for r in range(0, 4, 2):
                four = [None, None]
                for qq, rr in ((q, r), (q, r + 1), (q + 1, r), (q + 1, r + 1)):
                    couplings = fine_couplings(qq, rr)
                    for slot in slots:
                        left = source[slot, qq * 4 + rr] - OMEGA * field[0, slot, place(qq, rr)]
                        left = left + fine_coupled(couplings, (0, slot), qq, rr)
                        term = total[qq * 4 + rr] * left
                        four[slot] = term if four[slot] is None else four[slot] + term
                key = (q // 2, r // 2)
                for slot in slots:
                    rhs[slot][key] = kept(half, half_ref, 7, *key) * fine.pair_sum(four[slot])
        extra = [correction(rhs[slot]) for slot in slots]
        for slot in slots:
            for q, r in fine.cells():
                corrected = field[0, slot, place(q, r)] + extra[slot][q // 2, r // 2]
                field[0, slot, place(q, r)] = corrected
            close_ends(field, 0, slot)

    def relax(before, after):
        for q, r in fine.cells():
            couplings = fine_couplings(q, r)
            for slot in slots:
                value = (1.0 - OMEGA) * field[before, slot, place(q, r)]
                value = value + source[slot, q * 4 + r]
                value = value + fine_coupled(couplings, (before, slot), q, r)
                field[after, slot, place(q, r)] = value
        for slot in slots:
            close_ends(field, after, slot)

    def cycle(index, carry):
        correct()
        relax(0, 1)

        @pl.when(index < CYCLES - 1)
        def _():
            relax(1, 0)

        return carry

    lax.fori_loop(0, CYCLES, cycle, 0)
    for q in range(8):
        for slot in slots:
            turned = exchange_groups([field[1, slot, place(q, r)] for r in range(4)])
            for part in range(4):
                out_ref[part, slot, pl.ds(q, 8, stride=8), :] = turned[part]


def near(value):
    return pltpu.with_memory_space_constraint(value, pltpu.VMEM)


def in_scalars(value):
    return pltpu.with_memory_space_constraint(value, pltpu.SMEM)


def fill_table(owner, offsets_ref, counts_ref, shift_ref, table_ref):
    orbital_count = counts_ref.shape[0]
    core = owner & 1
    base = 2 * (owner - core) - 4

    def orbital_of(place):
        orbital = base + jnp.where(place < 2, 2 * core, 2) + place
        return jnp.where(orbital < 0, orbital + orbital_count, orbital)

    for slot in range(SLOTS):
        one = jnp.where(core == 0, ONE[0][slot], ONE[1][slot])
        other = jnp.where(core == 0, OTHER[0][slot], OTHER[1][slot])
        first, second = orbital_of(one), orbital_of(other)
        gap = second - first
        gap = jnp.where(gap < 0, gap + orbital_count, gap)
        live = jnp.int32(0)
        for rank in range(PMAX):
            listed = (counts_ref[first] > rank) & (offsets_ref[rank, first] + 1 == gap)
            live = live + listed.astype(jnp.int32)
        table_ref[DELTA + slot] = shift_ref[first] - shift_ref[second]
        table_ref[FIRST + slot] = one
        table_ref[SECOND + slot] = other
        table_ref[LIVE + slot] = live
    table_ref[CORE] = core


def prepare_kernel(
    own_hbm, eps_hbm, offsets_hbm, counts_hbm, shift_hbm,
    packet_ref, table_ref,
    offsets_ref, counts_ref, shift_ref, sems,
):
    copies = [
        pltpu.make_async_copy(offsets_hbm, offsets_ref, sems.at[0]),
        pltpu.make_async_copy(counts_hbm, counts_ref, sems.at[1]),
        pltpu.make_async_copy(shift_hbm, shift_ref, sems.at[2]),
        pltpu.make_async_copy(own_hbm, packet_ref.at[0:2], sems.at[3]),
        pltpu.make_async_copy(eps_hbm, packet_ref.at[2:4], sems.at[4]),
    ]
    for copy in copies:
        copy.start()
    for copy in copies[:3]:
        copy.wait()
    fill_table(lax.axis_index("orb"), offsets_ref, counts_ref, shift_ref, table_ref)
    for copy in copies[3:]:
        copy.wait()


def shards(orbitals, dielectric, pair_offsets, pair_counts, box_shift):
    owners = lax.axis_size("orb")

    swapped = [(source, source ^ 1) for source in range(owners)]
    onward = [(source, (source + 2) % owners) for source in range(owners)]
    backward = [(source, (source - 2) % owners) for source in range(owners)]

    own = as_rows(orbitals)
    eps = as_rows(dielectric)
    smem = pl.BlockSpec(memory_space=pltpu.SMEM)
    vmem = pl.BlockSpec(memory_space=pltpu.VMEM)
    anywhere = pl.BlockSpec(memory_space=pl.ANY)
    count = pair_counts.shape[0]
    packet, table = pl.pallas_call(
        prepare_kernel,
        out_shape=(
            pltpu.VMEM((4, ROWS, LANES), jnp.float32),
            pltpu.SMEM((4 * SLOTS + 1,), jnp.int32),
        ),
        in_specs=[anywhere] * 5,
        out_specs=(vmem, smem),
        scratch_shapes=[
            pltpu.SMEM((PMAX, count), jnp.int32),
            pltpu.SMEM((count,), jnp.int32),
            pltpu.SMEM((count,), jnp.int32),
            pltpu.SemaphoreType.DMA((5,)),
        ],
        name="pair_prepare",
    )(own, eps, pair_offsets.T, pair_counts, box_shift)
    table = in_scalars(table)
    before = lax.ppermute(packet, "orb", onward)
    across = lax.ppermute(own, "orb", swapped)
    pad_scratch = pltpu.VMEM((6, PADDED, 8, LANES), jnp.float32)
    requests = pl.pallas_call(
        pre_kernel,
        out_shape=pltpu.VMEM((4, 3, ROWS, LANES), jnp.float32),
        in_specs=[smem, vmem, vmem, vmem],
        out_specs=vmem,
        scratch_shapes=[pad_scratch],
        name="pair_sources",
    )(table, near(before), near(across), near(packet))
    arrived = lax.all_to_all(requests, "grid", 0, 0)
    cells = (32, 8, LANES)
    ended = (40, 8, LANES)
    potentials = pl.pallas_call(
        solve_kernel,
        out_shape=pltpu.VMEM((4, 2, ROWS, LANES), jnp.float32),
        in_specs=[vmem],
        out_specs=vmem,
        scratch_shapes=[
            pltpu.VMEM(ended, jnp.float32),
            pltpu.VMEM((6, *cells), jnp.float32),
            pltpu.VMEM(cells, jnp.float32),
            pltpu.VMEM((2, *cells), jnp.float32),
            pltpu.VMEM((2, 2, *ended), jnp.float32),
            pltpu.VMEM((8, 8, 8, LANES), jnp.float32),
            pltpu.VMEM((8, 2, 8, LANES), jnp.float32),
        ],
        name="pair_solve",
    )(near(arrived))
    returned = lax.all_to_all(potentials, "grid", 0, 0)
    two = pltpu.VMEM((2, ROWS, LANES), jnp.float32)
    for_before, for_across, mine = pl.pallas_call(
        post_kernel,
        out_shape=(two, two, two),
        in_specs=[smem, vmem, vmem, vmem, vmem],
        out_specs=(vmem, vmem, vmem),
        scratch_shapes=[
            pad_scratch,
            pltpu.VMEM((2, PADDED, 8, LANES), jnp.float32),
            pltpu.VMEM((6, ROWS, LANES), jnp.float32),
        ],
        name="pair_actions",
    )(table, near(before), near(across), near(packet), near(returned))
    from_next = lax.ppermute(for_before, "orb", backward)
    from_across = lax.ppermute(for_across, "orb", swapped)
    return from_rows(mine + from_across + from_next)


def solution(mesh):
    placed = (P("orb", "grid", None), P("orb", "grid", None), P(), P(), P())
    return jax.shard_map(
        shards, mesh=mesh, in_specs=placed, out_specs=P("orb", "grid", None), check_vma=False
    )
```

```python
import jax
import jax.numpy as jnp
from jax import lax
from jax.experimental import pallas as pl
from jax.experimental.pallas import tpu as pltpu
from jax.sharding import PartitionSpec as P

PMAX = 4
SMAX = 8
CYCLES = 2
SWEEPS = 4
FOURPI = 4.0 * 3.141592653589793
OMEGA = 0.8

SLOTS = 8
ONE = ((0, 0, 1, 1, 2, 2, 3, 3), (0, 0, 0, 0, 1, 1, 1, 1))
OTHER = ((1, 2, 2, 3, 4, 5, 4, 5), (1, 2, 3, 4, 2, 3, 4, 5))
DELTA, FIRST, SECOND, LIVE, CORE = 0, SLOTS, 2 * SLOTS, 3 * SLOTS, 4 * SLOTS
FRONT = 2
PADDED = 13
ROWS = 64
LANES = 128


def as_rows(value):
    count = value.shape[0]
    return value.reshape(count, 8, 8, LANES).transpose(0, 2, 1, 3).reshape(count, ROWS, LANES)


def from_rows(value):
    count = value.shape[0]
    return value.reshape(count, 8, 8, LANES).transpose(0, 2, 1, 3).reshape(count, 8, 8 * LANES)


def lane_of(shape):
    return lax.broadcasted_iota(jnp.int32, shape, len(shape) - 1)


def fill_padded(pad, place, source, index):
    for block in range(8):
        pad[place, FRONT + block] = source[index, 8 * block : 8 * block + 8, :]


def clear_margins(pad, count):
    nothing = jnp.zeros((8, LANES), jnp.float32)
    for place in range(count):
        for block in (0, 1, 10, 11, 12):
            pad[place, block] = nothing


def shifted(pad, place, delta):
    moved = delta + SMAX
    first = moved >> 2
    part = moved & 3
    turn = (LANES - 32 * part) & (LANES - 1)
    keep = lane_of((8, LANES)) < LANES - 32 * part
    rolled = [pltpu.roll(pad[place, first + block], turn, 1) for block in range(9)]
    return [jnp.where(keep, rolled[block], rolled[block + 1]) for block in range(8)]


def gather_fields(core, before_ref, across_ref, own_ref, pad):
    for index in range(2):
        fill_padded(pad, index, before_ref, index)
        fill_padded(pad, 2 + 2 * core + index, own_ref, index)
        fill_padded(pad, 4 - 2 * core + index, across_ref, index)
    clear_margins(pad, 6)


def pre_kernel(table_ref, before_ref, across_ref, own_ref, out_ref, pad):
    core = table_ref[CORE]
    gather_fields(core, before_ref, across_ref, own_ref, pad)
    for slot in range(SLOTS):
        one, other = table_ref[FIRST + slot], table_ref[SECOND + slot]
        moved = shifted(pad, other, table_ref[DELTA + slot])
        for block in range(8):
            out_ref[slot // 2, slot % 2, 8 * block : 8 * block + 8, :] = FOURPI * (
                pad[one, FRONT + block] * moved[block]
            )
    out_ref[0, 2] = before_ref[2]
    out_ref[1, 2] = before_ref[3 - core]
    out_ref[2, 2] = jnp.where(core == 0, own_ref[2], before_ref[3])
    out_ref[3, 2] = jnp.where(core == 0, own_ref[3], before_ref[3])


def post_kernel(
    table_ref, before_ref, across_ref, own_ref, pot_ref, before_out, across_out, own_out, pad, back, acc
):
    core = table_ref[CORE]
    gather_fields(core, before_ref, across_ref, own_ref, pad)
    clear_margins(back, 2)
    nothing = jnp.zeros((ROWS, LANES), jnp.float32)
    for place in range(6):
        acc[place] = nothing
    for slot in range(SLOTS):
        delta = table_ref[DELTA + slot]
        one, other = table_ref[FIRST + slot], table_ref[SECOND + slot]
        live = table_ref[LIVE + slot] > 0
        moved = shifted(pad, other, delta)
        for block in range(8):
            rows = slice(8 * block, 8 * block + 8)
            value = jnp.where(live, pot_ref[slot // 2, slot % 2, rows, :], 0.0)
            acc[one, rows, :] = acc[one, rows, :] - value * moved[block]
            back[slot % 2, FRONT + block] = value * pad[one, FRONT + block]
        returned = shifted(back, slot % 2, -delta)
        for block in range(8):
            rows = slice(8 * block, 8 * block + 8)
            acc[other, rows, :] = acc[other, rows, :] - returned[block]
    for index in range(2):
        before_out[index] = acc[index]
        own_out[index] = acc[2 + 2 * core + index]
        across_out[index] = acc[4 - 2 * core + index]


def roll(value, steps, axis):
    size = value.shape[axis]
    return pltpu.roll(value, steps % size, axis)


def exchange_groups(parts):
    lane = lane_of((8, LANES))
    low = lane < 64
    even = (lane & 32) == 0
    halves = [None] * 4
    for index in range(2):
        above, below = parts[index], parts[index + 2]
        crossed = roll(jnp.where(low, below, above), 64, 1)
        halves[index] = jnp.where(low, above, crossed)
        halves[index + 2] = jnp.where(low, crossed, below)
    result = [None] * 4
    for index in (0, 2):
        left, right = halves[index], halves[index + 1]
        result[index] = jnp.where(even, left, roll(right, 32, 1))
        result[index + 1] = jnp.where(even, roll(left, -32, 1), right)
    return result


class Level:
    def __init__(self, depth):
        self.zs = 8 >> depth
        self.ys = 4 >> depth
        self.step = 1 << depth
        lane = lane_of((8, LANES))
        sub = lax.broadcasted_iota(jnp.int32, (8, LANES), 0)
        column = lane & 31
        self.inside = (
            lane < 96,
            lane >= 32,
            sub < 7,
            sub > 0,
            column < 32 - self.step,
            column >= self.step,
        )

    def neighbours(self, get, q, r):
        ys = self.ys
        return (
            get(q + 1, r),
            get(q - 1, r),
            get(q, r + 1) if r < ys - 1 else roll(get(q, 0), -1, 0),
            get(q, r - 1) if r > 0 else roll(get(q, ys - 1), 1, 0),
            roll(get(q, r), -self.step, 1),
            roll(get(q, r), self.step, 1),
        )

    def wrapped(self, values):
        zs = self.zs

        def get(q, r):
            if q == zs:
                return roll(values[0, r], -32, 1)
            if q == -1:
                return roll(values[zs - 1, r], 32, 1)
            return values[q, r]

        return get

    def edges(self, q, r):
        return (
            self.inside[0] if q == self.zs - 1 else None,
            self.inside[1] if q == 0 else None,
            self.inside[2] if r == self.ys - 1 else None,
            self.inside[3] if r == 0 else None,
            self.inside[4],
            self.inside[5],
        )

    def coefficients(self, get, q, r):
        centre = get(q, r)
        edges = self.edges(q, r)
        around = [
            value if edge is None else jnp.where(edge, value, 0.0)
            for value, edge in zip(self.neighbours(get, q, r), edges)
        ]
        total = 6.0 * centre + sum(around[1:], around[0])
        scale = OMEGA / total
        couplings = []
        for value, edge in zip(around, edges):
            coupling = (centre + value) * scale
            couplings.append(coupling if edge is None else jnp.where(edge, coupling, 0.0))
        return couplings, total, scale

    def coupled(self, get, couplings, q, r):
        terms = [c * v for c, v in zip(couplings, self.neighbours(get, q, r))]
        return (terms[0] + terms[1]) + (terms[2] + terms[3]) + (terms[4] + terms[5])

    def pair_sum(self, value):
        even = (lane_of((8, LANES)) & self.step) == 0
        return value + jnp.where(even, roll(value, -self.step, 1), roll(value, self.step, 1))

    def block_sums(self, get):
        sums = {}
        for q in range(0, self.zs, 2):
            for r in range(0, self.ys, 2):
                four = (get(q, r) + get(q, r + 1)) + (get(q + 1, r) + get(q + 1, r + 1))
                sums[q // 2, r // 2] = self.pair_sum(four)
        return sums

    def cells(self):
        return [(q, r) for q in range(self.zs) for r in range(self.ys)]


def mixed_pair_sum(first, second):
    even = (lane_of((8, LANES)) & 1) == 0
    here = jnp.where(even, first, second)
    there = jnp.where(even, second, first)
    return here + jnp.where(even, roll(there, -1, 1), roll(there, 1, 1))


def unmixed(value):
    even = (lane_of((8, LANES)) & 1) == 0
    return (
        jnp.where(even, value, roll(value, 1, 1)),
        jnp.where(even, roll(value, -1, 1), value),
    )


def solve_kernel(in_ref, out_ref, eps, couple, total, source, field, half_ref, quarter_ref):
    fine, half, quarter = Level(0), Level(1), Level(2)
    slots = (0, 1)

    def place(q, r):
        return (q + 1) * 4 + r

    def at(ref, *lead):
        return lambda q, r: ref[(*lead, place(q, r))]

    def close_ends(ref, *lead):
        for r in range(4):
            ref[(*lead, place(8, r))] = roll(ref[(*lead, place(0, r))], -32, 1)
            ref[(*lead, place(-1, r))] = roll(ref[(*lead, place(7, r))], 32, 1)

    for q in range(8):
        for which in range(3):
            parts = [in_ref[part, which, pl.ds(q, 8, stride=8), :] for part in range(4)]
            turned = exchange_groups(parts)
            for r in range(4):
                if which == 2:
                    eps[place(q, r)] = turned[r]
                else:
                    source[which, q * 4 + r] = turned[r]
    close_ends(eps)

    get_eps = at(eps)
    for q, r in fine.cells():
        couplings, summed, scale = fine.coefficients(get_eps, q, r)
        for side in range(6):
            couple[side, q * 4 + r] = couplings[side]
        total[q * 4 + r] = summed
        for slot in slots:
            started = (2.0 * scale) * source[slot, q * 4 + r]
            source[slot, q * 4 + r] = started
            field[0, slot, place(q, r)] = started
    for slot in slots:
        close_ends(field, 0, slot)

    def keep_level(level, ref, eps_level):
        get = level.wrapped(eps_level)
        for q, r in level.cells():
            couplings, summed, scale = level.coefficients(get, q, r)
            for side in range(6):
                ref[side, q * level.ys + r] = couplings[side]
            ref[6, q * level.ys + r] = summed
            ref[7, q * level.ys + r] = 0.625 * scale

    def means(level, get):
        return {key: 0.125 * value for key, value in level.block_sums(get).items()}

    eps_half = means(fine, get_eps)
    keep_level(half, half_ref, eps_half)
    keep_level(quarter, quarter_ref, means(half, lambda q, r: eps_half[q, r]))

    def kept(level, ref, item, q, r):
        return ref[item, q * level.ys + r]

    def around(level, ref, values, q, r):
        couplings = [kept(level, ref, side, q, r) for side in range(6)]
        return level.coupled(level.wrapped(values), couplings, q, r)

    def relaxed(level, ref, values, rhs):
        return {
            (q, r): ((1.0 - OMEGA) * values[q, r] + rhs[q, r]) + around(level, ref, values, q, r)
            for q, r in level.cells()
        }

    def correction(rhs):
        def weighted(q, r):
            return kept(half, half_ref, 6, q, r) * (
                (1.0 - OMEGA) * rhs[q, r] + around(half, half_ref, rhs, q, r)
            )

        sums = half.block_sums(weighted)
        start = {key: kept(quarter, quarter_ref, 7, *key) * sums[key] for key in quarter.cells()}
        lowest = start
        for _ in range(SWEEPS - 1):
            lowest = relaxed(quarter, quarter_ref, lowest, start)
        values = {(q, r): rhs[q, r] + lowest[q // 2, r // 2] for q, r in half.cells()}
        return relaxed(half, half_ref, values, rhs)

    def fine_coupled(couplings, lead, q, r):
        return fine.coupled(at(field, *lead), couplings, q, r)

    def fine_couplings(q, r):
        return [couple[side, q * 4 + r] for side in range(6)]

    def correct():
        rhs = {}
        for q in range(0, 8, 2):
            for r in range(0, 4, 2):
                four = [None, None]
                for qq, rr in ((q, r), (q, r + 1), (q + 1, r), (q + 1, r + 1)):
                    couplings = fine_couplings(qq, rr)
                    for slot in slots:
                        left = source[slot, qq * 4 + rr] - OMEGA * field[0, slot, place(qq, rr)]
                        left = left + fine_coupled(couplings, (0, slot), qq, rr)
                        term = total[qq * 4 + rr] * left
                        four[slot] = term if four[slot] is None else four[slot] + term
                key = (q // 2, r // 2)
                rhs[key] = kept(half, half_ref, 7, *key) * mixed_pair_sum(*four)
        extra = {key: unmixed(value) for key, value in correction(rhs).items()}
        for slot in slots:
            for q, r in fine.cells():
                corrected = field[0, slot, place(q, r)] + extra[q // 2, r // 2][slot]
                field[0, slot, place(q, r)] = corrected
            close_ends(field, 0, slot)

    def relax(before, after):
        for q, r in fine.cells():
            couplings = fine_couplings(q, r)
            for slot in slots:
                value = (1.0 - OMEGA) * field[before, slot, place(q, r)]
                value = value + source[slot, q * 4 + r]
                value = value + fine_coupled(couplings, (before, slot), q, r)
                field[after, slot, place(q, r)] = value
        for slot in slots:
            close_ends(field, after, slot)

    def cycle(index, carry):
        correct()
        relax(0, 1)

        @pl.when(index < CYCLES - 1)
        def _():
            relax(1, 0)

        return carry

    lax.fori_loop(0, CYCLES, cycle, 0)
    for q in range(8):
        for slot in slots:
            turned = exchange_groups([field[1, slot, place(q, r)] for r in range(4)])
            for part in range(4):
                out_ref[part, slot, pl.ds(q, 8, stride=8), :] = turned[part]


def near(value):
    return pltpu.with_memory_space_constraint(value, pltpu.VMEM)


def in_scalars(value):
    return pltpu.with_memory_space_constraint(value, pltpu.SMEM)


def fill_table(owner, offsets_ref, counts_ref, shift_ref, table_ref):
    orbital_count = counts_ref.shape[0]
    core = owner & 1
    base = 2 * (owner - core) - 4

    def orbital_of(place):
        orbital = base + jnp.where(place < 2, 2 * core, 2) + place
        return jnp.where(orbital < 0, orbital + orbital_count, orbital)

    for slot in range(SLOTS):
        one = jnp.where(core == 0, ONE[0][slot], ONE[1][slot])
        other = jnp.where(core == 0, OTHER[0][slot], OTHER[1][slot])
        first, second = orbital_of(one), orbital_of(other)
        gap = second - first
        gap = jnp.where(gap < 0, gap + orbital_count, gap)
        live = jnp.int32(0)
        for rank in range(PMAX):
            listed = (counts_ref[first] > rank) & (offsets_ref[rank, first] + 1 == gap)
            live = live + listed.astype(jnp.int32)
        table_ref[DELTA + slot] = shift_ref[first] - shift_ref[second]
        table_ref[FIRST + slot] = one
        table_ref[SECOND + slot] = other
        table_ref[LIVE + slot] = live
    table_ref[CORE] = core


def table_kernel(offsets_ref, counts_ref, shift_ref, table_ref):
    fill_table(lax.axis_index("orb"), offsets_ref, counts_ref, shift_ref, table_ref)


def prepare_kernel(own_hbm, eps_hbm, packet_ref, sems):
    copies = [
        pltpu.make_async_copy(own_hbm, packet_ref.at[0:2], sems.at[0]),
        pltpu.make_async_copy(eps_hbm, packet_ref.at[2:4], sems.at[1]),
    ]
    for copy in copies:
        copy.start()
    for copy in copies:
        copy.wait()


def shards(orbitals, dielectric, pair_offsets, pair_counts, box_shift):
    owners = lax.axis_size("orb")

    swapped = [(source, source ^ 1) for source in range(owners)]
    onward = [(source, (source + 2) % owners) for source in range(owners)]
    backward = [(source, (source - 2) % owners) for source in range(owners)]

    own = as_rows(orbitals)
    eps = as_rows(dielectric)
    smem = pl.BlockSpec(memory_space=pltpu.SMEM)
    vmem = pl.BlockSpec(memory_space=pltpu.VMEM)
    anywhere = pl.BlockSpec(memory_space=pl.ANY)
    packet = pl.pallas_call(
        prepare_kernel,
        out_shape=pltpu.VMEM((4, ROWS, LANES), jnp.float32),
        in_specs=[anywhere] * 2,
        out_specs=vmem,
        scratch_shapes=[pltpu.SemaphoreType.DMA((2,))],
        name="pair_prepare",
    )(own, eps)
    before = lax.ppermute(packet, "orb", onward)
    across = lax.ppermute(own, "orb", swapped)
    table = pl.pallas_call(
        table_kernel,
        out_shape=pltpu.SMEM((4 * SLOTS + 1,), jnp.int32),
        in_specs=[smem, smem, smem],
        out_specs=smem,
        name="pair_table",
    )(pair_offsets.T, pair_counts, box_shift)
    table = in_scalars(table)
    pad_scratch = pltpu.VMEM((6, PADDED, 8, LANES), jnp.float32)
    requests = pl.pallas_call(
        pre_kernel,
        out_shape=pltpu.VMEM((4, 3, ROWS, LANES), jnp.float32),
        in_specs=[smem, vmem, vmem, vmem],
        out_specs=vmem,
        scratch_shapes=[pad_scratch],
        name="pair_sources",
    )(table, near(before), near(across), near(packet))
    arrived = lax.all_to_all(requests, "grid", 0, 0)
    cells = (32, 8, LANES)
    ended = (40, 8, LANES)
    potentials = pl.pallas_call(
        solve_kernel,
        out_shape=pltpu.VMEM((4, 2, ROWS, LANES), jnp.float32),
        in_specs=[vmem],
        out_specs=vmem,
        scratch_shapes=[
            pltpu.VMEM(ended, jnp.float32),
            pltpu.VMEM((6, *cells), jnp.float32),
            pltpu.VMEM(cells, jnp.float32),
            pltpu.VMEM((2, *cells), jnp.float32),
            pltpu.VMEM((2, 2, *ended), jnp.float32),
            pltpu.VMEM((8, 8, 8, LANES), jnp.float32),
            pltpu.VMEM((8, 2, 8, LANES), jnp.float32),
        ],
        name="pair_solve",
    )(near(arrived))
    returned = lax.all_to_all(potentials, "grid", 0, 0)
    two = pltpu.VMEM((2, ROWS, LANES), jnp.float32)
    for_before, for_across, mine = pl.pallas_call(
        post_kernel,
        out_shape=(two, two, two),
        in_specs=[smem, vmem, vmem, vmem, vmem],
        out_specs=(vmem, vmem, vmem),
        scratch_shapes=[
            pad_scratch,
            pltpu.VMEM((2, PADDED, 8, LANES), jnp.float32),
            pltpu.VMEM((6, ROWS, LANES), jnp.float32),
        ],
        name="pair_actions",
    )(table, near(before), near(across), near(packet), near(returned))
    from_next = lax.ppermute(for_before, "orb", backward)
    from_across = lax.ppermute(for_across, "orb", swapped)
    return from_rows(mine + from_across + from_next)


def solution(mesh):
    placed = (P("orb", "grid", None), P("orb", "grid", None), P(), P(), P())
    return jax.shard_map(
        shards, mesh=mesh, in_specs=placed, out_specs=P("orb", "grid", None), check_vma=False
    )
```
